32 devices in a mesh: dp: 8 (over y, x, core), tensor: 4 (over z).
Axes of the slice: x: 2, y: 2, z: 4, core: 2. Of those that a mesh axis runs over, the one named last changes fastest.
Arguments:
- hidden_in: bfloat16 [8, 1024, 1024], P('dp', 'tensor'), may hold values from -40 to 40
- segment_ids: int32 [8, 1024], P('dp'), may hold values from 0 to 1024, as said below
- gain_attn: float32 [1024], replicated, may hold values from 0.25 to 1.75
- gain_mlp: float32 [1024], replicated, may hold values from 0.25 to 1.75
- w_qkv: bfloat16 [1024, 3, 1024], P(None, None, 'tensor'), may hold values from -3 to 3
- w_out: bfloat16 [1024, 1024], P('tensor'), may hold values from -0.75 to 0.75
- w_in: bfloat16 [1024, 2, 2624], P(None, None, 'tensor'), may hold values from -0.1875 to 0.1875
- w_down: bfloat16 [2624, 1024], P('tensor'), may hold values from -0.125 to 0.125
- out_grad: bfloat16 [8, 1024, 1024], P('dp', 'tensor'), may hold values from -24 to 24
Outputs:
- hidden_out: bfloat16 [8, 1024, 1024], P('dp', 'tensor')
- hidden_grad: float32 [8, 1024, 1024], P('dp', 'tensor')
- gain_attn_grad: float32 [1024], P('tensor')
- gain_mlp_grad: float32 [1024], P('tensor')
- w_qkv_grad: float32 [1024, 3, 1024], P(None, None, 'tensor')
- w_out_grad: float32 [1024, 1024], P('tensor')
- w_in_grad: float32 [1024, 2, 2624], P(None, None, 'tensor')
- w_down_grad: float32 [2624, 1024], P('tensor')
The draws below stay inside these ranges and needn't reach their ends.
Inputs may be any that keep to these rules, and one draw needn't show every extreme that they name: `segment_ids`: within a group the ids never fall along the slots; documents carry ids 0, 1, 2 and so on in order; the id 1024 marks padding, which fills the last slots of every group, one or more of them.
All inputs are finite; a program needn't handle non-finite values.
Results may differ from the reference program's by a relative error of at most 0.035.
Values may be sent and summed in bfloat16 or wider, within the bound.
A program may use at most 128 MiB of HBM per device.

```python
import math
import jax
import jax.numpy as jnp
from jax import lax

D = 1024
HEADS = 16
HEAD_DIM = 64
FF = 2624
LEN_MAX = 512
GROUP_TOK = 1024
GROUPS = 8
N_TENSOR = 4


def draw_hidden_in(key, part):
    base_key = jax.random.fold_in(key, 11)
    col_key = jax.random.fold_in(base_key, 0)
    main_key = jax.random.fold_in(base_key, 2)
    col_scale = jnp.exp(jax.random.uniform(col_key, (D,), jnp.float32, math.log(0.3), math.log(3.0)))
    main_draw = jnp.clip(jax.random.normal(main_key, (GROUPS, GROUP_TOK, D), jnp.float32), -6.0, 6.0)
    field_vals = main_draw * col_scale
    return field_vals.astype(jnp.bfloat16)


def draw_segment_ids(key, part):
    base_key = jax.random.fold_in(key, 23)
    len_key, fill_key = jax.random.split(base_key, 2)
    doc_lens = jax.random.randint(len_key, (GROUPS, GROUP_TOK), 1, LEN_MAX + 1, dtype=jnp.int32)
    doc_lens = doc_lens.at[:, 0].set(jnp.maximum(doc_lens[:, 0], 4))
    doc_ends = jnp.cumsum(doc_lens, axis=1)
    token_idx = jnp.arange(GROUP_TOK, dtype=jnp.int32)
    seg_vals = jax.vmap(lambda ends_row: jnp.searchsorted(ends_row, token_idx, side='right'))(doc_ends).astype(jnp.int32)
    fill_len = jax.random.randint(fill_key, (GROUPS, 1), GROUP_TOK // 2, GROUP_TOK - 15, dtype=jnp.int32)
    return jnp.where(token_idx[None, :] < fill_len, seg_vals, GROUP_TOK).astype(jnp.int32)


def draw_w_qkv(key, part):
    base_vals = jnp.clip(jax.random.normal(jax.random.fold_in(key, 31), (D, 3, D), jnp.float32), -6.0, 6.0) * (1.0 / math.sqrt(D))
    return base_vals.astype(jnp.bfloat16)


def draw_out_grad(key, part):
    base_key = jax.random.fold_in(key, 41)
    main_key = jax.random.fold_in(base_key, 0)
    row_pos = jnp.arange(GROUPS * GROUP_TOK, dtype=jnp.float32).reshape(GROUPS, GROUP_TOK, 1)
    rise_vals = 1.0 + 2.0 * row_pos / (GROUPS * GROUP_TOK - 1)
    main_draw = jnp.clip(jax.random.normal(main_key, (GROUPS, GROUP_TOK, D), jnp.float32), -6.0, 6.0)
    grad_vals = main_draw * rise_vals
    return grad_vals.astype(jnp.bfloat16)


def block_scale(own_key, shape, pieces, least, top_value):
    factor_of = 1.0
    for position, blocks in pieces:
        draws = jax.random.uniform(jax.random.fold_in(jax.random.fold_in(own_key, 6), position), (blocks,), jnp.float32, least / len(pieces), top_value / len(pieces))
        factor_of = factor_of * jnp.repeat(jnp.exp(draws), shape[position] // blocks).reshape((-1,) + (1,) * (len(shape) - 1 - position))
    return factor_of


def gaussian(own_key, shape, scale, reach, cuts=(), held_as=jnp.bfloat16):
    values = scale * jax.random.normal(own_key, shape, jnp.float32)
    if cuts:
        values = values * block_scale(own_key, shape, cuts, -0.22, 0.18)
    return jnp.clip(values, -reach, reach).astype(held_as)


def setup_inputs(seed: int = 0) -> dict:
    arg_keys = jax.random.split(jax.random.key(seed), 10)
    return {
        "hidden_in": draw_hidden_in(jax.random.fold_in(arg_keys[9], 71), 0),
        "segment_ids": draw_segment_ids(jax.random.fold_in(arg_keys[9], 71), 0),
        "gain_attn": jnp.clip(1.0 + 0.15 * jax.random.normal(arg_keys[2], (D,), jnp.float32), 0.25, 1.75),
        "gain_mlp": jnp.clip(1.0 + 0.15 * jax.random.normal(arg_keys[3], (D,), jnp.float32), 0.25, 1.75),
        "w_qkv": draw_w_qkv(jax.random.fold_in(arg_keys[9], 71), 0),
        "w_out": gaussian(arg_keys[5], (D, D), 64 ** -0.5, 0.75, ((0, 4),)),
        "w_in": gaussian(arg_keys[6], (D, 2, FF), D ** -0.5, 0.1875, ((2, 4),)),
        "w_down": gaussian(arg_keys[7], (FF, D), FF ** -0.5, 0.125, ((0, 4),)),
        "out_grad": draw_out_grad(jax.random.fold_in(arg_keys[9], 71), 0),
    }


eps_norm = 1e-05
rope_theta = 160000.0
neg_fill = -1e+30
sqrt_half = 0.7071067811865476
inv_sqrt_two_pi = 0.3989422804014327

def norm_fwd(rows_f, gain_vec):
    mean_row = lax.optimization_barrier(jnp.mean(rows_f, axis=-1, keepdims=True))
    centred = rows_f - mean_row
    var_row = lax.optimization_barrier(jnp.mean(centred * centred, axis=-1, keepdims=True))
    inv_std = lax.rsqrt(var_row + eps_norm)
    hat_rows = centred * inv_std
    return ((hat_rows * gain_vec).astype(jnp.bfloat16), hat_rows, inv_std)

def norm_bwd(grad_norm, hat_rows, inv_std, gain_vec):
    grad_hat = grad_norm * gain_vec
    mean_one = lax.optimization_barrier(jnp.mean(grad_hat, axis=-1, keepdims=True))
    mean_two = lax.optimization_barrier(jnp.mean(grad_hat * hat_rows, axis=-1, keepdims=True))
    return inv_std * (grad_hat - mean_one - hat_rows * mean_two)

def half_turn(field_in):
    half_dim = field_in.shape[-1] // 2
    return jnp.concatenate([-field_in[..., half_dim:], field_in[..., :half_dim]], axis=-1)

def positions_of(seg_row):
    before = lax.optimization_barrier(jnp.sum((seg_row[None, :] < seg_row[:, None]).astype(jnp.int32), axis=1))
    return jnp.arange(seg_row.shape[0], dtype=jnp.int32) - before

def rope_tables(positions, head_dim):
    half_dim = head_dim // 2
    inv_freq = jnp.exp(jnp.arange(half_dim, dtype=jnp.float32) * (-2.0 * math.log(rope_theta) / head_dim))
    angles = positions.astype(jnp.float32)[:, None] * inv_freq[None, :]
    cos_tab = jnp.concatenate([jnp.cos(angles), jnp.cos(angles)], axis=-1)
    sin_tab = jnp.concatenate([jnp.sin(angles), jnp.sin(angles)], axis=-1)
    return (cos_tab[:, None, :], sin_tab[:, None, :])

def rope_apply(field_in, cos_tab, sin_tab):
    return field_in * cos_tab + half_turn(field_in) * sin_tab

def rope_back(grad_in, cos_tab, sin_tab):
    return grad_in * cos_tab - half_turn(grad_in * sin_tab)

def gelu_val(field_in):
    return 0.5 * field_in * (1.0 + lax.erf(field_in * sqrt_half))

def gelu_slope(field_in):
    return 0.5 * (1.0 + lax.erf(field_in * sqrt_half)) + field_in * jnp.exp(-0.5 * field_in * field_in) * inv_sqrt_two_pi

def blocked_sum(left, right, spec):
    parts = jnp.einsum(spec, left.astype(jnp.float32), right.astype(jnp.float32))
    rounded = lax.optimization_barrier(parts.astype(jnp.bfloat16))
    return lax.optimization_barrier(jnp.sum(rounded.astype(jnp.float32), axis=0))

def attend_fwd(queries, key_rows, value_rows, seg_row):
    total_rows = queries.shape[0]
    block_rows = min(512, total_rows)
    scale_val = 1.0 / math.sqrt(queries.shape[2])
    key_f = key_rows.astype(jnp.float32)
    value_f = value_rows.astype(jnp.float32)

    def one_block(block_idx):
        start_row = block_idx * block_rows
        query_blk = lax.dynamic_slice_in_dim(queries, start_row, block_rows, 0).astype(jnp.float32)
        seg_blk = lax.dynamic_slice_in_dim(seg_row, start_row, block_rows, 0)
        scores = jnp.einsum('qhd,khd->hqk', query_blk, key_f) * scale_val
        same_doc = seg_blk[:, None] == seg_row[None, :]
        scores = jnp.where(same_doc[None], scores, neg_fill)
        row_top = lax.optimization_barrier(jnp.max(scores, axis=-1, keepdims=True))
        exp_vals = jnp.exp(scores - row_top)
        row_total = lax.optimization_barrier(jnp.sum(exp_vals, axis=-1, keepdims=True))
        prob_bf = (exp_vals / row_total).astype(jnp.bfloat16)
        out_blk = jnp.einsum('hqk,khd->qhd', prob_bf.astype(jnp.float32), value_f).astype(jnp.bfloat16)
        return (out_blk, (row_top + jnp.log(row_total))[..., 0])
    out_blocks, lse_blocks = lax.map(one_block, jnp.arange(total_rows // block_rows, dtype=jnp.int32))
    head_count = queries.shape[1]
    att_out = out_blocks.reshape(total_rows, head_count, queries.shape[2])
    lse_rows = jnp.transpose(lse_blocks, (1, 0, 2)).reshape(head_count, total_rows)
    return (att_out, lse_rows)

def attend_bwd(queries, key_rows, value_rows, seg_row, att_out, grad_att, lse_rows):
    total_rows = queries.shape[0]
    block_rows = min(512, total_rows)
    scale_val = 1.0 / math.sqrt(queries.shape[2])
    key_f = key_rows.astype(jnp.float32)
    value_f = value_rows.astype(jnp.float32)
    delta_rows = lax.optimization_barrier(jnp.sum(grad_att.astype(jnp.float32) * att_out.astype(jnp.float32), axis=-1))

    def one_block(acc_pair, block_idx):
        grad_key, grad_value = acc_pair
        start_row = block_idx * block_rows
        query_blk = lax.dynamic_slice_in_dim(queries, start_row, block_rows, 0).astype(jnp.float32)
        grad_blk = lax.dynamic_slice_in_dim(grad_att, start_row, block_rows, 0).astype(jnp.float32)
        seg_blk = lax.dynamic_slice_in_dim(seg_row, start_row, block_rows, 0)
        delta_blk = lax.dynamic_slice_in_dim(delta_rows, start_row, block_rows, 0)
        lse_blk = lax.dynamic_slice_in_dim(lse_rows, start_row, block_rows, 1)
        scores = jnp.einsum('qhd,khd->hqk', query_blk, key_f) * scale_val
        same_doc = seg_blk[:, None] == seg_row[None, :]
        scores = jnp.where(same_doc[None], scores, neg_fill)
        prob_f = jnp.exp(scores - lse_blk[:, :, None])
        grad_prob = jnp.einsum('qhd,khd->hqk', grad_blk, value_f)
        grad_score = prob_f * (grad_prob - jnp.transpose(delta_blk)[:, :, None])
        prob_bf = prob_f.astype(jnp.bfloat16).astype(jnp.float32)
        score_bf = grad_score.astype(jnp.bfloat16).astype(jnp.float32)
        grad_value = grad_value + jnp.einsum('hqk,qhd->khd', prob_bf, grad_blk)
        grad_key = grad_key + jnp.einsum('hqk,qhd->khd', score_bf, query_blk) * scale_val
        grad_query_blk = jnp.einsum('hqk,khd->qhd', score_bf, key_f) * scale_val
        return ((grad_key, grad_value), grad_query_blk)
    zero_rows = jnp.zeros(key_rows.shape, jnp.float32)
    acc_pair, query_blocks = lax.scan(one_block, (zero_rows, zero_rows), jnp.arange(total_rows // block_rows, dtype=jnp.int32))
    return (query_blocks.reshape(queries.shape), acc_pair[0], acc_pair[1])

def reference(hidden_in, segment_ids, gain_attn, gain_mlp, w_qkv, w_out, w_in, w_down, out_grad):
    n_parts = N_TENSOR
    width_local = D // n_parts
    ff_local = FF // n_parts
    total_rows = GROUP_TOK

    def group_step(carried, group_items):
        rows_in, seg_row, grad_rows = group_items
        positions = positions_of(seg_row)
        cos_tab, sin_tab = rope_tables(positions, HEAD_DIM)
        valid_rows = (seg_row < GROUP_TOK).astype(jnp.float32)
        rows_f = rows_in.astype(jnp.float32)
        normed_attn, hat_attn, inv_attn = norm_fwd(rows_f, gain_attn)
        projected = jnp.dot(normed_attn, w_qkv.reshape(D, 3 * D), preferred_element_type=jnp.float32)
        projected = projected.reshape(total_rows, 3, HEADS, HEAD_DIM)
        queries = rope_apply(projected[:, 0], cos_tab, sin_tab).astype(jnp.bfloat16)
        key_rows = rope_apply(projected[:, 1], cos_tab, sin_tab).astype(jnp.bfloat16)
        value_rows = projected[:, 2].astype(jnp.bfloat16)
        att_out, lse_rows = attend_fwd(queries, key_rows, value_rows, seg_row)
        att_flat = att_out.reshape(total_rows, D)
        att_sum = blocked_sum(att_flat.reshape(total_rows, n_parts, width_local), w_out.reshape(n_parts, width_local, D), 'snk,nkd->nsd')
        mid_rows = rows_f + att_sum
        normed_mlp, hat_mlp, inv_mlp = norm_fwd(mid_rows, gain_mlp)
        pre_act = jnp.dot(normed_mlp, w_in.reshape(D, 2 * FF), preferred_element_type=jnp.float32).reshape(total_rows, 2, FF)
        up_part = pre_act[:, 0]
        gate_part = pre_act[:, 1]
        act_up = gelu_val(up_part)
        mixed_act = (act_up * gate_part).astype(jnp.bfloat16)
        mlp_sum = blocked_sum(mixed_act.reshape(total_rows, n_parts, ff_local), w_down.reshape(n_parts, ff_local, D), 'snk,nkd->nsd')
        final_rows = (mid_rows + mlp_sum).astype(jnp.bfloat16)
        grad_top = grad_rows.astype(jnp.float32) * valid_rows[:, None]
        grad_top_bf = grad_top.astype(jnp.bfloat16)
        grad_down = jnp.dot(mixed_act.T, grad_top_bf, preferred_element_type=jnp.float32)
        d_mixed = jnp.dot(grad_top_bf, w_down.T, preferred_element_type=jnp.float32)
        d_up = d_mixed * gate_part * gelu_slope(up_part)
        d_gate = d_mixed * act_up
        d_pre = jnp.stack([d_up, d_gate], axis=1).astype(jnp.bfloat16)
        grad_in = jnp.dot(normed_mlp.T, d_pre.reshape(total_rows, 2 * FF), preferred_element_type=jnp.float32).reshape(D, 2, FF)
        d_norm_mlp = blocked_sum(d_pre.reshape(total_rows, 2, n_parts, ff_local), w_in.reshape(D, 2, n_parts, ff_local), 'scnf,dcnf->nsd')
        gain_mlp_part = lax.optimization_barrier(jnp.sum(d_norm_mlp * hat_mlp, axis=0))
        d_mid = grad_top + norm_bwd(d_norm_mlp, hat_mlp, inv_mlp, gain_mlp)
        d_mid_bf = d_mid.astype(jnp.bfloat16)
        grad_out_w = jnp.dot(att_flat.T, d_mid_bf, preferred_element_type=jnp.float32)
        d_att = jnp.dot(d_mid_bf, w_out.T, preferred_element_type=jnp.float32).astype(jnp.bfloat16)
        d_att = d_att.reshape(total_rows, HEADS, HEAD_DIM)
        grad_query, grad_key, grad_value = attend_bwd(queries, key_rows, value_rows, seg_row, att_out, d_att, lse_rows)
        grad_query = rope_back(grad_query, cos_tab, sin_tab)
        grad_key = rope_back(grad_key, cos_tab, sin_tab)
        d_proj = jnp.stack([grad_query, grad_key, grad_value], axis=1).reshape(total_rows, 3, D).astype(jnp.bfloat16)
        grad_qkv = jnp.dot(normed_attn.T, d_proj.reshape(total_rows, 3 * D), preferred_element_type=jnp.float32).reshape(D, 3, D)
        d_norm_attn = blocked_sum(d_proj.reshape(total_rows, 3, n_parts, width_local), w_qkv.reshape(D, 3, n_parts, width_local), 'scnf,dcnf->nsd')
        gain_attn_part = lax.optimization_barrier(jnp.sum(d_norm_attn * hat_attn, axis=0))
        d_rows = d_mid + norm_bwd(d_norm_attn, hat_attn, inv_attn, gain_attn)
        acc_qkv, acc_out, acc_in, acc_down, acc_gain_attn, acc_gain_mlp = carried
        carried = (acc_qkv + grad_qkv, acc_out + grad_out_w, acc_in + grad_in, acc_down + grad_down, acc_gain_attn + gain_attn_part, acc_gain_mlp + gain_mlp_part)
        return (carried, (final_rows, d_rows))
    start_acc = (jnp.zeros((D, 3, D), jnp.float32), jnp.zeros((D, D), jnp.float32), jnp.zeros((D, 2, FF), jnp.float32), jnp.zeros((FF, D), jnp.float32), jnp.zeros((D,), jnp.float32), jnp.zeros((D,), jnp.float32))
    carried, (outs_all, grads_all) = lax.scan(group_step, start_acc, (hidden_in, segment_ids, out_grad))
    acc_qkv, acc_out, acc_in, acc_down, acc_gain_attn, acc_gain_mlp = carried
    return (outs_all, grads_all, acc_gain_attn, acc_gain_mlp, acc_qkv, acc_out, acc_in, acc_down)
```

```python
import functools
import math

import jax
import jax.numpy as jnp
from jax import lax
from jax.experimental import pallas as pl
from jax.experimental.pallas import tpu as pltpu
from jax.sharding import PartitionSpec as P

HEAD_DIM = 64


eps_norm = 1e-05
rope_theta = 160000.0
neg_fill = -1e30
sqrt_half = 0.7071067811865476
inv_sqrt_two_pi = 0.3989422804014327


def norm_fwd(rows_f, gain_vec):
    mean_row = jnp.mean(rows_f, axis=-1, keepdims=True)
    centred = rows_f - mean_row
    var_row = jnp.mean(centred * centred, axis=-1, keepdims=True)
    inv_std = lax.rsqrt(var_row + eps_norm)
    hat_rows = centred * inv_std
    return ((hat_rows * gain_vec).astype(jnp.bfloat16), hat_rows, inv_std)


def norm_bwd(grad_norm, hat_rows, inv_std, gain_vec):
    grad_hat = grad_norm * gain_vec
    mean_one = jnp.mean(grad_hat, axis=-1, keepdims=True)
    mean_two = jnp.mean(grad_hat * hat_rows, axis=-1, keepdims=True)
    return inv_std * (grad_hat - mean_one - hat_rows * mean_two)


def half_turn(field_in):
    half_dim = field_in.shape[-1] // 2
    return jnp.concatenate([-field_in[..., half_dim:], field_in[..., :half_dim]], axis=-1)


def positions_of(seg_row):
    before = jnp.sum((seg_row[None, :] < seg_row[:, None]).astype(jnp.int32), axis=1)
    return jnp.arange(seg_row.shape[0], dtype=jnp.int32) - before


def rope_tables(positions, head_dim):
    half_dim = head_dim // 2
    inv_freq = jnp.exp(
        jnp.arange(half_dim, dtype=jnp.float32) * (-2.0 * math.log(rope_theta) / head_dim)
    )
    angles = positions.astype(jnp.float32)[:, None] * inv_freq[None, :]
    cos_tab = jnp.concatenate([jnp.cos(angles), jnp.cos(angles)], axis=-1)
    sin_tab = jnp.concatenate([jnp.sin(angles), jnp.sin(angles)], axis=-1)
    return (cos_tab[:, None, :], sin_tab[:, None, :])


def rope_apply(field_in, cos_tab, sin_tab):
    return field_in * cos_tab + half_turn(field_in) * sin_tab


def rope_back(grad_in, cos_tab, sin_tab):
    return grad_in * cos_tab - half_turn(grad_in * sin_tab)


def gelu_val(field_in):
    return 0.5 * field_in * (1.0 + lax.erf(field_in * sqrt_half))


def gelu_slope(field_in):
    return (
        0.5 * (1.0 + lax.erf(field_in * sqrt_half))
        + field_in * jnp.exp(-0.5 * field_in * field_in) * inv_sqrt_two_pi
    )


def attend_fwd(queries, key_rows, value_rows, seg_row):
    total_rows = queries.shape[0]
    block_rows = min(512, total_rows)
    scale_val = 1.0 / math.sqrt(queries.shape[2])

    def one_block(block_idx):
        start_row = block_idx * block_rows
        query_blk = lax.dynamic_slice_in_dim(queries, start_row, block_rows, 0)
        seg_blk = lax.dynamic_slice_in_dim(seg_row, start_row, block_rows, 0)
        scores = (
            jnp.einsum("qhd,khd->hqk", query_blk, key_rows, preferred_element_type=jnp.float32)
            * scale_val
        )
        same_doc = seg_blk[:, None] == seg_row[None, :]
        scores = jnp.where(same_doc[None], scores, neg_fill)
        row_top = jnp.max(scores, axis=-1, keepdims=True)
        exp_vals = jnp.exp(scores - row_top)
        row_total = jnp.sum(exp_vals, axis=-1, keepdims=True)
        prob_bf = (exp_vals / row_total).astype(jnp.bfloat16)
        out_blk = jnp.einsum(
            "hqk,khd->qhd", prob_bf, value_rows, preferred_element_type=jnp.float32
        ).astype(jnp.bfloat16)
        return (out_blk, (row_top + jnp.log(row_total))[..., 0])

    out_blocks, lse_blocks = lax.map(
        one_block, jnp.arange(total_rows // block_rows, dtype=jnp.int32)
    )
    head_count = queries.shape[1]
    att_out = out_blocks.reshape(total_rows, head_count, queries.shape[2])
    lse_rows = jnp.transpose(lse_blocks, (1, 0, 2)).reshape(head_count, total_rows)
    return (att_out, lse_rows)


def attend_bwd(queries, key_rows, value_rows, seg_row, att_out, grad_att, lse_rows):
    total_rows = queries.shape[0]
    block_rows = min(512, total_rows)
    scale_val = 1.0 / math.sqrt(queries.shape[2])
    delta_rows = jnp.sum(grad_att.astype(jnp.float32) * att_out.astype(jnp.float32), axis=-1)

    def one_block(acc_pair, block_idx):
        grad_key, grad_value = acc_pair
        start_row = block_idx * block_rows
        query_blk = lax.dynamic_slice_in_dim(queries, start_row, block_rows, 0)
        grad_blk = lax.dynamic_slice_in_dim(grad_att, start_row, block_rows, 0)
        seg_blk = lax.dynamic_slice_in_dim(seg_row, start_row, block_rows, 0)
        delta_blk = lax.dynamic_slice_in_dim(delta_rows, start_row, block_rows, 0)
        lse_blk = lax.dynamic_slice_in_dim(lse_rows, start_row, block_rows, 1)
        scores = (
            jnp.einsum("qhd,khd->hqk", query_blk, key_rows, preferred_element_type=jnp.float32)
            * scale_val
        )
        same_doc = seg_blk[:, None] == seg_row[None, :]
        scores = jnp.where(same_doc[None], scores, neg_fill)
        prob_f = jnp.exp(scores - lse_blk[:, :, None])
        grad_prob = jnp.einsum(
            "qhd,khd->hqk", grad_blk, value_rows, preferred_element_type=jnp.float32
        )
        grad_score = prob_f * (grad_prob - jnp.transpose(delta_blk)[:, :, None])
        prob_bf = prob_f.astype(jnp.bfloat16)
        score_bf = grad_score.astype(jnp.bfloat16)
        grad_value = grad_value + jnp.einsum(
            "hqk,qhd->khd", prob_bf, grad_blk, preferred_element_type=jnp.float32
        )
        grad_key = (
            grad_key
            + jnp.einsum("hqk,qhd->khd", score_bf, query_blk, preferred_element_type=jnp.float32)
            * scale_val
        )
        grad_query_blk = (
            jnp.einsum("hqk,khd->qhd", score_bf, key_rows, preferred_element_type=jnp.float32)
            * scale_val
        )
        return ((grad_key, grad_value), grad_query_blk)

    zero_rows = jnp.zeros(key_rows.shape, jnp.float32)
    acc_pair, query_blocks = lax.scan(
        one_block, (zero_rows, zero_rows), jnp.arange(total_rows // block_rows, dtype=jnp.int32)
    )
    return (query_blocks.reshape(queries.shape), acc_pair[0], acc_pair[1])


def bit_orders(n_dp):
    bits = [1 << i for i in range(n_dp.bit_length() - 1)]
    rest = bits[1:]
    turn = len(rest) // 2
    return (bits, bits[:1] + rest[turn:] + rest[:turn])


def grad_reduce_kernel(n_dp, n_arr, *refs):
    orders = bit_orders(n_dp)
    n_stage = len(orders[0])
    x_refs = refs[:n_arr]
    out_refs = refs[n_arr : 2 * n_arr]
    pos = 2 * n_arr
    gath = refs[pos : pos + n_arr]
    pos += n_arr
    recv = [refs[pos + s * n_arr : pos + (s + 1) * n_arr] for s in range(n_stage)]
    pos += n_stage * n_arr
    work = [refs[pos + s * n_arr : pos + (s + 1) * n_arr] for s in range(n_stage - 1)]
    pos += (n_stage - 1) * n_arr
    send_sem, recv_sem = refs[pos], refs[pos + 1]
    me = lax.axis_index("dp")
    mine = lax.axis_index("tensor")

    def bit_of(bit):
        return lax.rem(me // bit, 2)

    def partner_of(bit):
        return me + bit - 2 * bit * bit_of(bit)

    def remote(src, dst, step, half, arr, bit):
        return pltpu.make_async_remote_copy(
            src_ref=src,
            dst_ref=dst,
            send_sem=send_sem.at[step, half, arr],
            recv_sem=recv_sem.at[step, half, arr],
            device_id=(partner_of(bit), mine),
            device_id_type=pl.DeviceIdType.MESH,
        )

    barrier = pltpu.get_barrier_semaphore()
    for bit in orders[0]:
        pl.semaphore_signal(
            barrier, inc=1, device_id=(partner_of(bit), mine), device_id_type=pl.DeviceIdType.MESH
        )
    pl.semaphore_wait(barrier, n_stage)

    offs = [[0], [0]]
    for stage in range(n_stage):
        size = n_dp >> (stage + 1)
        copies = []
        for half in range(2):
            bit = orders[half][stage]
            offs[half].append(offs[half][-1] + bit_of(bit) * size)
            for arr in range(n_arr):
                src = x_refs[arr] if stage == 0 else work[stage - 1][arr]
                away = (1 - bit_of(bit)) * size
                copies.append(
                    remote(
                        src.at[half, pl.ds(away, size)],
                        recv[stage][arr].at[half],
                        stage,
                        half,
                        arr,
                        bit,
                    )
                )
                copies[-1].start()
        for half in range(2):
            kept = bit_of(orders[half][stage]) * size
            for arr in range(n_arr):
                copies[half * n_arr + arr].wait_recv()
                src = x_refs[arr] if stage == 0 else work[stage - 1][arr]
                last = stage == n_stage - 1
                base = offs[half][-1] if last else 0
                dst = gath[arr] if last else work[stage][arr]

                def add_one(i, carry, src=src, dst=dst, kept=kept, base=base, half=half, arr=arr):
                    total = src[half, kept + i].astype(jnp.float32) + recv[stage][arr][
                        half, i
                    ].astype(jnp.float32)
                    dst[half, base + i] = total.astype(jnp.bfloat16)
                    return carry

                lax.fori_loop(0, size, add_one, 0)
        for copy in copies:
            copy.wait_send()
    for stage in reversed(range(n_stage)):
        size = n_dp >> (stage + 1)
        copies = []
        for half in range(2):
            bit = orders[half][stage]
            start = offs[half][stage + 1]
            for arr in range(n_arr):
                part = gath[arr].at[half, pl.ds(start, size)]
                copies.append(remote(part, part, n_stage + stage, half, arr, bit))
                copies[-1].start()
        for copy in copies:
            copy.wait()
    for arr in range(n_arr):
        for half in range(2):

            def move_one(i, carry, arr=arr, half=half):
                out_refs[arr][half, i] = gath[arr][half, i]
                return carry

            lax.fori_loop(0, n_dp, move_one, 0)


def grad_reduce(grads, call_id):
    n_dp = lax.axis_size("dp")
    rows = grads[0].shape[0]
    if n_dp < 4 or n_dp & (n_dp - 1) or rows % (2 * n_dp):
        return [lax.psum(g.astype(jnp.bfloat16), "dp") for g in grads]
    n_arr = len(grads)
    n_stage = n_dp.bit_length() - 1
    part = rows // (2 * n_dp)
    cols = [g.shape[1] for g in grads]
    args = [g.astype(jnp.bfloat16).reshape(2, n_dp, part, c) for g, c in zip(grads, cols)]
    scratch = [pltpu.VMEM((2, n_dp, part, c), jnp.bfloat16) for c in cols]
    for stage in range(n_stage):
        scratch += [pltpu.VMEM((2, n_dp >> (stage + 1), part, c), jnp.bfloat16) for c in cols]
    for stage in range(n_stage - 1):
        scratch += [pltpu.VMEM((2, n_dp >> (stage + 1), part, c), jnp.bfloat16) for c in cols]
    scratch += [pltpu.SemaphoreType.DMA((2 * n_stage, 2, n_arr))] * 2
    moved = 2 * sum(rows * c for c in cols)
    outs = pl.pallas_call(
        functools.partial(grad_reduce_kernel, n_dp, n_arr),
        out_shape=[jax.ShapeDtypeStruct(a.shape, jnp.bfloat16) for a in args],
        in_specs=[pl.BlockSpec(memory_space=pltpu.VMEM)] * n_arr,
        out_specs=[pl.BlockSpec(memory_space=pltpu.VMEM)] * n_arr,
        scratch_shapes=scratch,
        cost_estimate=pl.CostEstimate(flops=0, bytes_accessed=30 * moved, transcendentals=0),
        compiler_params=pltpu.CompilerParams(
            collective_id=call_id, has_side_effects=True, vmem_limit_bytes=40 << 20
        ),
    )(*args)
    return [o.reshape(rows, c) for o, c in zip(outs, cols)]


def shards(hidden_in, segment_ids, gain_attn, gain_mlp, w_qkv, w_out, w_in, w_down, out_grad):
    n_parts = lax.axis_size("tensor")
    shard_rows = hidden_in.shape[1]
    total_rows = shard_rows * n_parts
    model_width = hidden_in.shape[2]
    width_local = w_qkv.shape[2]
    head_local = width_local // HEAD_DIM
    ff_local = w_in.shape[2]
    my_index = lax.axis_index("tensor")
    seg_row = segment_ids[0]
    positions = positions_of(seg_row)
    cos_tab, sin_tab = rope_tables(positions, HEAD_DIM)
    my_seg = lax.dynamic_slice_in_dim(seg_row, my_index * shard_rows, shard_rows, 0)
    valid_rows = (my_seg < total_rows).astype(jnp.float32)
    rows_f = hidden_in[0].astype(jnp.float32)
    normed_attn, hat_attn, inv_attn = norm_fwd(rows_f, gain_attn)
    gathered_attn = lax.all_gather(normed_attn, "tensor", axis=0, tiled=True)
    grad_top = out_grad[0].astype(jnp.float32) * valid_rows[:, None]
    gathered_attn, grad_top_bf = lax.optimization_barrier(
        (gathered_attn, grad_top.astype(jnp.bfloat16))
    )
    grad_all = lax.all_gather(grad_top_bf, "tensor", axis=0, tiled=True)
    projected = jnp.dot(
        gathered_attn,
        w_qkv.reshape(model_width, 3 * width_local),
        preferred_element_type=jnp.float32,
    )
    projected = projected.reshape(total_rows, 3, head_local, HEAD_DIM)
    queries = rope_apply(projected[:, 0], cos_tab, sin_tab).astype(jnp.bfloat16)
    key_rows = rope_apply(projected[:, 1], cos_tab, sin_tab).astype(jnp.bfloat16)
    value_rows = projected[:, 2].astype(jnp.bfloat16)
    att_out, lse_rows = attend_fwd(queries, key_rows, value_rows, seg_row)
    att_flat = att_out.reshape(total_rows, width_local)
    att_part = jnp.dot(att_flat, w_out, preferred_element_type=jnp.float32).astype(jnp.bfloat16)
    att_part, grad_all = lax.optimization_barrier((att_part, grad_all))
    att_sum = lax.psum_scatter(
        att_part,
        "tensor",
        scatter_dimension=0,
        tiled=True,
    ).astype(jnp.float32)
    mid_rows = rows_f + att_sum
    normed_mlp, hat_mlp, inv_mlp = norm_fwd(mid_rows, gain_mlp)
    gathered_mlp = lax.all_gather(normed_mlp, "tensor", axis=0, tiled=True)
    pre_act = jnp.dot(
        gathered_mlp, w_in.reshape(model_width, 2 * ff_local), preferred_element_type=jnp.float32
    )
    pre_act = pre_act.reshape(total_rows, 2, ff_local)
    up_part = pre_act[:, 0]
    gate_part = pre_act[:, 1]
    act_up = gelu_val(up_part)
    mixed_act = (act_up * gate_part).astype(jnp.bfloat16)
    mlp_part = jnp.dot(mixed_act, w_down, preferred_element_type=jnp.float32).astype(jnp.bfloat16)
    d_mixed = lax.dot_general(
        grad_all, w_down, (((1,), (1,)), ((), ())), preferred_element_type=jnp.float32
    )
    d_up = d_mixed * gate_part * gelu_slope(up_part)
    d_gate = d_mixed * act_up
    d_pre = jnp.stack([d_up, d_gate], axis=1).astype(jnp.bfloat16)
    d_norm_part = lax.dot_general(
        d_pre, w_in, (((1, 2), (1, 2)), ((), ())), preferred_element_type=jnp.float32
    ).astype(jnp.bfloat16)
    d_norm_part, d_pre = lax.optimization_barrier((d_norm_part, d_pre))
    d_norm_mlp = lax.psum_scatter(d_norm_part, "tensor", scatter_dimension=0, tiled=True)
    grad_in = lax.dot_general(
        gathered_mlp,
        d_pre.reshape(total_rows, 2 * ff_local),
        (((0,), (0,)), ((), ())),
        preferred_element_type=jnp.float32,
    ).astype(jnp.bfloat16)
    grad_down = lax.dot_general(
        grad_all, mixed_act, (((0,), (0,)), ((), ())), preferred_element_type=jnp.float32
    ).astype(jnp.bfloat16)
    d_norm_mlp, grad_in, grad_down, mlp_part = lax.optimization_barrier(
        (d_norm_mlp, grad_in, grad_down, mlp_part)
    )
    d_norm_mlp = d_norm_mlp.astype(jnp.float32)
    gain_mlp_part = jnp.sum(d_norm_mlp * hat_mlp, axis=0)
    d_mid = grad_top + norm_bwd(d_norm_mlp, hat_mlp, inv_mlp, gain_mlp)
    d_mid_bf, grad_in, grad_down = lax.optimization_barrier(
        (d_mid.astype(jnp.bfloat16), grad_in, grad_down)
    )
    d_mid_all = lax.all_gather(d_mid_bf, "tensor", axis=0, tiled=True)
    grad_in, grad_down = grad_reduce([grad_in, grad_down], 0)
    d_mid_all, grad_in, grad_down, mlp_part = lax.optimization_barrier(
        (d_mid_all, grad_in, grad_down, mlp_part)
    )
    mlp_sum = lax.psum_scatter(mlp_part, "tensor", scatter_dimension=0, tiled=True)
    d_att = lax.dot_general(
        d_mid_all, w_out, (((1,), (1,)), ((), ())), preferred_element_type=jnp.float32
    )
    d_att = d_att.astype(jnp.bfloat16).reshape(total_rows, head_local, HEAD_DIM)
    grad_query, grad_key, grad_value = attend_bwd(
        queries, key_rows, value_rows, seg_row, att_out, d_att, lse_rows
    )
    grad_query = rope_back(grad_query, cos_tab, sin_tab)
    grad_key = rope_back(grad_key, cos_tab, sin_tab)
    d_proj = (
        jnp.stack([grad_query, grad_key, grad_value], axis=1)
        .reshape(total_rows, 3, width_local)
        .astype(jnp.bfloat16)
    )
    d_attn_part = lax.dot_general(
        d_proj, w_qkv, (((1, 2), (1, 2)), ((), ())), preferred_element_type=jnp.float32
    ).astype(jnp.bfloat16)
    d_attn_part, mlp_sum, d_proj = lax.optimization_barrier((d_attn_part, mlp_sum, d_proj))
    final_rows = (mid_rows + mlp_sum.astype(jnp.float32)).astype(jnp.bfloat16)
    d_norm_attn = lax.psum_scatter(d_attn_part, "tensor", scatter_dimension=0, tiled=True)
    grad_qkv = lax.dot_general(
        gathered_attn,
        d_proj.reshape(total_rows, 3 * width_local),
        (((0,), (0,)), ((), ())),
        preferred_element_type=jnp.float32,
    )
    grad_out_w = lax.dot_general(
        d_mid_all, att_flat, (((0,), (0,)), ((), ())), preferred_element_type=jnp.float32
    )
    grad_qkv, grad_out_w = grad_reduce([grad_qkv, grad_out_w], 1)
    d_norm_attn, grad_qkv, grad_out_w = lax.optimization_barrier(
        (d_norm_attn, grad_qkv, grad_out_w)
    )
    d_norm_attn = d_norm_attn.astype(jnp.float32)
    gain_attn_part = jnp.sum(d_norm_attn * hat_attn, axis=0)
    d_rows = d_mid + norm_bwd(d_norm_attn, hat_attn, inv_attn, gain_attn)
    gain_both = lax.psum_scatter(
        jnp.stack([gain_attn_part, gain_mlp_part]), "tensor", scatter_dimension=1, tiled=True
    )
    gain_both = lax.psum(gain_both, "dp")
    grad_qkv = grad_qkv.astype(jnp.float32).reshape(model_width, 3, width_local)
    grad_in = grad_in.astype(jnp.float32).reshape(model_width, 2, ff_local)
    grad_out_w = jnp.transpose(grad_out_w.astype(jnp.float32))
    grad_down = jnp.transpose(grad_down.astype(jnp.float32))
    return (
        final_rows[None],
        d_rows[None],
        gain_both[0],
        gain_both[1],
        grad_qkv,
        grad_out_w,
        grad_in,
        grad_down,
    )


def solution(mesh):
    return jax.shard_map(
        shards,
        mesh=mesh,
        in_specs=(
            P("dp", "tensor", None),
            P("dp", None),
            P(),
            P(),
            P(None, None, "tensor"),
            P("tensor", None),
            P(None, None, "tensor"),
            P("tensor", None),
            P("dp", "tensor", None),
        ),
        out_specs=(
            P("dp", "tensor", None),
            P("dp", "tensor", None),
            P("tensor"),
            P("tensor"),
            P(None, None, "tensor"),
            P("tensor", None),
            P(None, None, "tensor"),
            P("tensor", None),
        ),
        check_vma=False,
    )
```

```python
import functools
import math

import jax
import jax.numpy as jnp
from jax import lax
from jax.experimental import pallas as pl
from jax.experimental.pallas import tpu as pltpu
from jax.sharding import PartitionSpec as P

HEAD_DIM = 64


eps_norm = 1e-05
rope_theta = 160000.0
neg_fill = -1e30
sqrt_half = 0.7071067811865476
inv_sqrt_two_pi = 0.3989422804014327


def norm_fwd(rows_f, gain_vec):
    mean_row = jnp.mean(rows_f, axis=-1, keepdims=True)
    centred = rows_f - mean_row
    var_row = jnp.mean(centred * centred, axis=-1, keepdims=True)
    inv_std = lax.rsqrt(var_row + eps_norm)
    hat_rows = centred * inv_std
    return ((hat_rows * gain_vec).astype(jnp.bfloat16), hat_rows, inv_std)


def norm_bwd(grad_norm, hat_rows, inv_std, gain_vec):
    grad_hat = grad_norm * gain_vec
    mean_one = jnp.mean(grad_hat, axis=-1, keepdims=True)
    mean_two = jnp.mean(grad_hat * hat_rows, axis=-1, keepdims=True)
    return inv_std * (grad_hat - mean_one - hat_rows * mean_two)


def half_turn(field_in):
    half_dim = field_in.shape[-1] // 2
    return jnp.concatenate([-field_in[..., half_dim:], field_in[..., :half_dim]], axis=-1)


def positions_of(seg_row):
    before = jnp.sum((seg_row[None, :] < seg_row[:, None]).astype(jnp.int32), axis=1)
    return jnp.arange(seg_row.shape[0], dtype=jnp.int32) - before


def rope_tables(positions, head_dim):
    half_dim = head_dim // 2
    inv_freq = jnp.exp(
        jnp.arange(half_dim, dtype=jnp.float32) * (-2.0 * math.log(rope_theta) / head_dim)
    )
    angles = positions.astype(jnp.float32)[:, None] * inv_freq[None, :]
    cos_tab = jnp.concatenate([jnp.cos(angles), jnp.cos(angles)], axis=-1)
    sin_tab = jnp.concatenate([jnp.sin(angles), jnp.sin(angles)], axis=-1)
    return (cos_tab[:, None, :], sin_tab[:, None, :])


def rope_apply(field_in, cos_tab, sin_tab):
    return field_in * cos_tab + half_turn(field_in) * sin_tab


def rope_back(grad_in, cos_tab, sin_tab):
    return grad_in * cos_tab - half_turn(grad_in * sin_tab)


def gelu_val(field_in):
    return 0.5 * field_in * (1.0 + lax.erf(field_in * sqrt_half))


def gelu_slope(field_in):
    return (
        0.5 * (1.0 + lax.erf(field_in * sqrt_half))
        + field_in * jnp.exp(-0.5 * field_in * field_in) * inv_sqrt_two_pi
    )


def attend_fwd(queries, key_rows, value_rows, seg_row):
    total_rows = queries.shape[0]
    block_rows = min(512, total_rows)
    scale_val = 1.0 / math.sqrt(queries.shape[2])

    def one_block(block_idx):
        start_row = block_idx * block_rows
        query_blk = lax.dynamic_slice_in_dim(queries, start_row, block_rows, 0)
        seg_blk = lax.dynamic_slice_in_dim(seg_row, start_row, block_rows, 0)
        scores = (
            jnp.einsum("qhd,khd->hqk", query_blk, key_rows, preferred_element_type=jnp.float32)
            * scale_val
        )
        same_doc = seg_blk[:, None] == seg_row[None, :]
        scores = jnp.where(same_doc[None], scores, neg_fill)
        row_top = jnp.max(scores, axis=-1, keepdims=True)
        exp_vals = jnp.exp(scores - row_top)
        row_total = jnp.sum(exp_vals, axis=-1, keepdims=True)
        prob_bf = (exp_vals / row_total).astype(jnp.bfloat16)
        out_blk = jnp.einsum(
            "hqk,khd->qhd", prob_bf, value_rows, preferred_element_type=jnp.float32
        ).astype(jnp.bfloat16)
        return (out_blk, (row_top + jnp.log(row_total))[..., 0])

    out_blocks, lse_blocks = lax.map(
        one_block, jnp.arange(total_rows // block_rows, dtype=jnp.int32)
    )
    head_count = queries.shape[1]
    att_out = out_blocks.reshape(total_rows, head_count, queries.shape[2])
    lse_rows = jnp.transpose(lse_blocks, (1, 0, 2)).reshape(head_count, total_rows)
    return (att_out, lse_rows)


def attend_bwd(queries, key_rows, value_rows, seg_row, att_out, grad_att, lse_rows):
    total_rows = queries.shape[0]
    block_rows = min(512, total_rows)
    scale_val = 1.0 / math.sqrt(queries.shape[2])
    delta_rows = jnp.sum(grad_att.astype(jnp.float32) * att_out.astype(jnp.float32), axis=-1)

    def one_block(acc_pair, block_idx):
        grad_key, grad_value = acc_pair
        start_row = block_idx * block_rows
        query_blk = lax.dynamic_slice_in_dim(queries, start_row, block_rows, 0)
        grad_blk = lax.dynamic_slice_in_dim(grad_att, start_row, block_rows, 0)
        seg_blk = lax.dynamic_slice_in_dim(seg_row, start_row, block_rows, 0)
        delta_blk = lax.dynamic_slice_in_dim(delta_rows, start_row, block_rows, 0)
        lse_blk = lax.dynamic_slice_in_dim(lse_rows, start_row, block_rows, 1)
        scores = (
            jnp.einsum("qhd,khd->hqk", query_blk, key_rows, preferred_element_type=jnp.float32)
            * scale_val
        )
        same_doc = seg_blk[:, None] == seg_row[None, :]
        scores = jnp.where(same_doc[None], scores, neg_fill)
        prob_f = jnp.exp(scores - lse_blk[:, :, None])
        grad_prob = jnp.einsum(
            "qhd,khd->hqk", grad_blk, value_rows, preferred_element_type=jnp.float32
        )
        grad_score = prob_f * (grad_prob - jnp.transpose(delta_blk)[:, :, None])
        prob_bf = prob_f.astype(jnp.bfloat16)
        score_bf = grad_score.astype(jnp.bfloat16)
        grad_value = grad_value + jnp.einsum(
            "hqk,qhd->khd", prob_bf, grad_blk, preferred_element_type=jnp.float32
        )
        grad_key = (
            grad_key
            + jnp.einsum("hqk,qhd->khd", score_bf, query_blk, preferred_element_type=jnp.float32)
            * scale_val
        )
        grad_query_blk = (
            jnp.einsum("hqk,khd->qhd", score_bf, key_rows, preferred_element_type=jnp.float32)
            * scale_val
        )
        return ((grad_key, grad_value), grad_query_blk)

    zero_rows = jnp.zeros(key_rows.shape, jnp.float32)
    acc_pair, query_blocks = lax.scan(
        one_block, (zero_rows, zero_rows), jnp.arange(total_rows // block_rows, dtype=jnp.int32)
    )
    return (query_blocks.reshape(queries.shape), acc_pair[0], acc_pair[1])


def bit_orders(n_dp):
    bits = [1 << i for i in range(n_dp.bit_length() - 1)]
    rest = bits[1:]
    turn = len(rest) // 2
    return (bits, bits[:1] + rest[turn:] + rest[:turn])


def grad_reduce_kernel(n_dp, n_arr, *refs):
    orders = bit_orders(n_dp)
    n_stage = len(orders[0])
    x_refs = refs[:n_arr]
    out_refs = refs[n_arr : 2 * n_arr]
    pos = 2 * n_arr
    gath = refs[pos : pos + n_arr]
    pos += n_arr
    recv = [refs[pos + s * n_arr : pos + (s + 1) * n_arr] for s in range(n_stage)]
    pos += n_stage * n_arr
    work = [refs[pos + s * n_arr : pos + (s + 1) * n_arr] for s in range(n_stage - 1)]
    pos += (n_stage - 1) * n_arr
    send_sem, recv_sem = refs[pos], refs[pos + 1]
    me = lax.axis_index("dp")
    mine = lax.axis_index("tensor")

    def bit_of(bit):
        return lax.rem(me // bit, 2)

    def partner_of(bit):
        return me + bit - 2 * bit * bit_of(bit)

    def remote(src, dst, step, half, arr, bit):
        return pltpu.make_async_remote_copy(
            src_ref=src,
            dst_ref=dst,
            send_sem=send_sem.at[step, half, arr],
            recv_sem=recv_sem.at[step, half, arr],
            device_id=(partner_of(bit), mine),
            device_id_type=pl.DeviceIdType.MESH,
        )

    barrier = pltpu.get_barrier_semaphore()
    for bit in orders[0]:
        pl.semaphore_signal(
            barrier, inc=1, device_id=(partner_of(bit), mine), device_id_type=pl.DeviceIdType.MESH
        )
    pl.semaphore_wait(barrier, n_stage)

    offs = [[0], [0]]
    for stage in range(n_stage):
        size = n_dp >> (stage + 1)
        copies = []
        for half in range(2):
            bit = orders[half][stage]
            offs[half].append(offs[half][-1] + bit_of(bit) * size)
            for arr in range(n_arr):
                src = x_refs[arr] if stage == 0 else work[stage - 1][arr]
                away = (1 - bit_of(bit)) * size
                copies.append(
                    remote(
                        src.at[half, pl.ds(away, size)],
                        recv[stage][arr].at[half],
                        stage,
                        half,
                        arr,
                        bit,
                    )
                )
                copies[-1].start()
        for half in range(2):
            kept = bit_of(orders[half][stage]) * size
            for arr in range(n_arr):
                copies[half * n_arr + arr].wait_recv()
                src = x_refs[arr] if stage == 0 else work[stage - 1][arr]
                last = stage == n_stage - 1
                base = offs[half][-1] if last else 0
                dst = gath[arr] if last else work[stage][arr]

                def add_one(i, carry, src=src, dst=dst, kept=kept, base=base, half=half, arr=arr):
                    total = src[half, kept + i].astype(jnp.float32) + recv[stage][arr][
                        half, i
                    ].astype(jnp.float32)
                    dst[half, base + i] = total.astype(jnp.bfloat16)
                    return carry

                lax.fori_loop(0, size, add_one, 0)
        for copy in copies:
            copy.wait_send()
    for stage in reversed(range(n_stage)):
        size = n_dp >> (stage + 1)
        copies = []
        for half in range(2):
            bit = orders[half][stage]
            start = offs[half][stage + 1]
            for arr in range(n_arr):
                part = gath[arr].at[half, pl.ds(start, size)]
                copies.append(remote(part, part, n_stage + stage, half, arr, bit))
                copies[-1].start()
        for copy in copies:
            copy.wait()
    for arr in range(n_arr):
        for half in range(2):

            def move_one(i, carry, arr=arr, half=half):
                out_refs[arr][half, i] = gath[arr][half, i]
                return carry

            lax.fori_loop(0, n_dp, move_one, 0)


def grad_reduce(grads, call_id):
    n_dp = lax.axis_size("dp")
    rows = grads[0].shape[0]
    if n_dp < 4 or n_dp & (n_dp - 1) or rows % (2 * n_dp):
        return [lax.psum(g.astype(jnp.bfloat16), "dp") for g in grads]
    n_arr = len(grads)
    n_stage = n_dp.bit_length() - 1
    part = rows // (2 * n_dp)
    cols = [g.shape[1] for g in grads]
    args = [g.astype(jnp.bfloat16).reshape(2, n_dp, part, c) for g, c in zip(grads, cols)]
    scratch = [pltpu.VMEM((2, n_dp, part, c), jnp.bfloat16) for c in cols]
    for stage in range(n_stage):
        scratch += [pltpu.VMEM((2, n_dp >> (stage + 1), part, c), jnp.bfloat16) for c in cols]
    for stage in range(n_stage - 1):
        scratch += [pltpu.VMEM((2, n_dp >> (stage + 1), part, c), jnp.bfloat16) for c in cols]
    scratch += [pltpu.SemaphoreType.DMA((2 * n_stage, 2, n_arr))] * 2
    moved = 2 * sum(rows * c for c in cols)
    outs = pl.pallas_call(
        functools.partial(grad_reduce_kernel, n_dp, n_arr),
        out_shape=[jax.ShapeDtypeStruct(a.shape, jnp.bfloat16) for a in args],
        in_specs=[pl.BlockSpec(memory_space=pltpu.VMEM)] * n_arr,
        out_specs=[pl.BlockSpec(memory_space=pltpu.VMEM)] * n_arr,
        scratch_shapes=scratch,
        cost_estimate=pl.CostEstimate(flops=0, bytes_accessed=30 * moved, transcendentals=0),
        compiler_params=pltpu.CompilerParams(
            collective_id=call_id, has_side_effects=True, vmem_limit_bytes=40 << 20
        ),
    )(*args)
    return [o.reshape(rows, c) for o, c in zip(outs, cols)]


def gain_reduce_kernel(n_dp, n_tp, x_ref, out_ref, stage_buf, from_tp, from_dp, t_send, t_recv, d_send, d_recv, c_sem):
    me = lax.axis_index("dp")
    mine = lax.axis_index("tensor")
    mesh_type = pl.DeviceIdType.MESH
    barrier = pltpu.get_barrier_semaphore()
    for k in range(1, n_tp):
        pl.semaphore_signal(
            barrier, inc=1, device_id=(me, lax.rem(mine + k, n_tp)), device_id_type=mesh_type
        )
    for k in range(1, n_dp):
        pl.semaphore_signal(
            barrier, inc=1, device_id=(lax.rem(me + k, n_dp), mine), device_id_type=mesh_type
        )
    pl.semaphore_wait(barrier, n_tp + n_dp - 2)
    copies = []
    for k in range(1, n_tp):
        target = lax.rem(mine + k, n_tp)
        copies.append(
            pltpu.make_async_remote_copy(
                src_ref=x_ref.at[target],
                dst_ref=from_tp.at[k],
                send_sem=t_send.at[k],
                recv_sem=t_recv.at[k],
                device_id=(me, target),
                device_id_type=mesh_type,
            )
        )
        copies[-1].start()
    total = x_ref[mine]
    for k in range(1, n_tp):
        copies[k - 1].wait()
        total = total + from_tp[k]
    stage_buf[...] = total
    local = pltpu.make_async_copy(stage_buf, from_dp.at[0], c_sem)
    local.start()
    local.wait()
    copies = []
    for k in range(1, n_dp):
        copies.append(
            pltpu.make_async_remote_copy(
                src_ref=from_dp.at[0],
                dst_ref=from_dp.at[k],
                send_sem=d_send.at[k],
                recv_sem=d_recv.at[k],
                device_id=(lax.rem(me + k, n_dp), mine),
                device_id_type=mesh_type,
            )
        )
        copies[-1].start()
    for k in range(1, n_dp):
        copies[k - 1].wait()
        total = total + from_dp[k]
    out_ref[...] = total


def gain_reduce(parts, call_id):
    n_dp = lax.axis_size("dp")
    n_tp = lax.axis_size("tensor")
    wide = parts.shape[1] // n_tp
    arg = jnp.transpose(parts.reshape(2, n_tp, wide), (1, 0, 2))
    return pl.pallas_call(
        functools.partial(gain_reduce_kernel, n_dp, n_tp),
        out_shape=jax.ShapeDtypeStruct((2, wide), jnp.float32),
        in_specs=[pl.BlockSpec(memory_space=pltpu.VMEM)],
        out_specs=pl.BlockSpec(memory_space=pltpu.VMEM),
        scratch_shapes=[
            pltpu.VMEM((2, wide), jnp.float32),
            pltpu.VMEM((n_tp, 2, wide), jnp.float32),
            pltpu.VMEM((n_dp, 2, wide), jnp.float32),
            pltpu.SemaphoreType.DMA((n_tp,)),
            pltpu.SemaphoreType.DMA((n_tp,)),
            pltpu.SemaphoreType.DMA((n_dp,)),
            pltpu.SemaphoreType.DMA((n_dp,)),
            pltpu.SemaphoreType.DMA,
        ],
        cost_estimate=pl.CostEstimate(flops=0, bytes_accessed=20 << 20, transcendentals=0),
        compiler_params=pltpu.CompilerParams(collective_id=call_id, has_side_effects=True),
    )(arg)


def shards(hidden_in, segment_ids, gain_attn, gain_mlp, w_qkv, w_out, w_in, w_down, out_grad):
    n_parts = lax.axis_size("tensor")
    shard_rows = hidden_in.shape[1]
    total_rows = shard_rows * n_parts
    model_width = hidden_in.shape[2]
    width_local = w_qkv.shape[2]
    head_local = width_local // HEAD_DIM
    ff_local = w_in.shape[2]
    my_index = lax.axis_index("tensor")
    seg_row = segment_ids[0]
    positions = positions_of(seg_row)
    cos_tab, sin_tab = rope_tables(positions, HEAD_DIM)
    my_seg = lax.dynamic_slice_in_dim(seg_row, my_index * shard_rows, shard_rows, 0)
    valid_rows = (my_seg < total_rows).astype(jnp.float32)
    rows_f = hidden_in[0].astype(jnp.float32)
    normed_attn, hat_attn, inv_attn = norm_fwd(rows_f, gain_attn)
    normed_attn, out_grad = lax.optimization_barrier((normed_attn, out_grad))
    gathered_attn = lax.all_gather(normed_attn, "tensor", axis=0, tiled=True)
    grad_top = out_grad[0].astype(jnp.float32) * valid_rows[:, None]
    grad_all = lax.all_gather(grad_top.astype(jnp.bfloat16), "tensor", axis=0, tiled=True)
    projected = jnp.dot(
        gathered_attn,
        w_qkv.reshape(model_width, 3 * width_local),
        preferred_element_type=jnp.float32,
    )
    projected = projected.reshape(total_rows, 3, head_local, HEAD_DIM)
    queries = rope_apply(projected[:, 0], cos_tab, sin_tab).astype(jnp.bfloat16)
    key_rows = rope_apply(projected[:, 1], cos_tab, sin_tab).astype(jnp.bfloat16)
    value_rows = projected[:, 2].astype(jnp.bfloat16)
    att_out, lse_rows = attend_fwd(queries, key_rows, value_rows, seg_row)
    att_flat = att_out.reshape(total_rows, width_local)
    att_part = jnp.dot(att_flat, w_out, preferred_element_type=jnp.float32).astype(jnp.bfloat16)
    att_part, grad_all = lax.optimization_barrier((att_part, grad_all))
    att_sum = lax.psum_scatter(
        att_part,
        "tensor",
        scatter_dimension=0,
        tiled=True,
    ).astype(jnp.float32)
    mid_rows = rows_f + att_sum
    normed_mlp, hat_mlp, inv_mlp = norm_fwd(mid_rows, gain_mlp)
    gathered_mlp = lax.all_gather(normed_mlp, "tensor", axis=0, tiled=True)
    pre_act = jnp.dot(
        gathered_mlp, w_in.reshape(model_width, 2 * ff_local), preferred_element_type=jnp.float32
    )
    pre_act = pre_act.reshape(total_rows, 2, ff_local)
    up_part = pre_act[:, 0]
    gate_part = pre_act[:, 1]
    act_up = gelu_val(up_part)
    mixed_act = (act_up * gate_part).astype(jnp.bfloat16)
    mlp_part = jnp.dot(mixed_act, w_down, preferred_element_type=jnp.float32).astype(jnp.bfloat16)
    d_mixed = lax.dot_general(
        grad_all, w_down, (((1,), (1,)), ((), ())), preferred_element_type=jnp.float32
    )
    d_up = d_mixed * gate_part * gelu_slope(up_part)
    d_gate = d_mixed * act_up
    d_pre = jnp.stack([d_up, d_gate], axis=1).astype(jnp.bfloat16)
    d_norm_part = lax.dot_general(
        d_pre, w_in, (((1, 2), (1, 2)), ((), ())), preferred_element_type=jnp.float32
    ).astype(jnp.bfloat16)
    d_norm_part, d_pre = lax.optimization_barrier((d_norm_part, d_pre))
    d_norm_mlp = lax.psum_scatter(d_norm_part, "tensor", scatter_dimension=0, tiled=True)
    grad_down = lax.dot_general(
        grad_all, mixed_act, (((0,), (0,)), ((), ())), preferred_element_type=jnp.float32
    ).astype(jnp.bfloat16)
    (grad_down,) = grad_reduce([grad_down], 2)
    grad_in = lax.dot_general(
        gathered_mlp,
        d_pre.reshape(total_rows, 2 * ff_local),
        (((0,), (0,)), ((), ())),
        preferred_element_type=jnp.float32,
    ).astype(jnp.bfloat16)
    d_norm_mlp, grad_in, grad_down, mlp_part = lax.optimization_barrier(
        (d_norm_mlp, grad_in, grad_down, mlp_part)
    )
    d_norm_mlp = d_norm_mlp.astype(jnp.float32)
    gain_mlp_part = jnp.sum(d_norm_mlp * hat_mlp, axis=0)
    d_mid = grad_top + norm_bwd(d_norm_mlp, hat_mlp, inv_mlp, gain_mlp)
    d_mid_bf, grad_in, mlp_part = lax.optimization_barrier(
        (d_mid.astype(jnp.bfloat16), grad_in, mlp_part)
    )
    d_mid_all = lax.all_gather(d_mid_bf, "tensor", axis=0, tiled=True)
    mlp_sum = lax.psum_scatter(mlp_part, "tensor", scatter_dimension=0, tiled=True)
    (grad_in,) = grad_reduce([grad_in], 0)
    grad_down = jnp.transpose(grad_down.astype(jnp.float32))
    d_mid_all, grad_in, grad_down = lax.optimization_barrier((d_mid_all, grad_in, grad_down))
    d_att = lax.dot_general(
        d_mid_all, w_out, (((1,), (1,)), ((), ())), preferred_element_type=jnp.float32
    )
    d_att = d_att.astype(jnp.bfloat16).reshape(total_rows, head_local, HEAD_DIM)
    grad_query, grad_key, grad_value = attend_bwd(
        queries, key_rows, value_rows, seg_row, att_out, d_att, lse_rows
    )
    grad_query = rope_back(grad_query, cos_tab, sin_tab)
    grad_key = rope_back(grad_key, cos_tab, sin_tab)
    d_proj = (
        jnp.stack([grad_query, grad_key, grad_value], axis=1)
        .reshape(total_rows, 3, width_local)
        .astype(jnp.bfloat16)
    )
    d_attn_part = lax.dot_general(
        d_proj, w_qkv, (((1, 2), (1, 2)), ((), ())), preferred_element_type=jnp.float32
    ).astype(jnp.bfloat16)
    d_attn_part, mlp_sum, d_proj = lax.optimization_barrier((d_attn_part, mlp_sum, d_proj))
    final_rows = (mid_rows + mlp_sum.astype(jnp.float32)).astype(jnp.bfloat16)
    d_norm_attn = lax.psum_scatter(d_attn_part, "tensor", scatter_dimension=0, tiled=True)
    grad_qkv = lax.dot_general(
        gathered_attn,
        d_proj.reshape(total_rows, 3 * width_local),
        (((0,), (0,)), ((), ())),
        preferred_element_type=jnp.float32,
    )
    grad_out_w = lax.dot_general(
        d_mid_all, att_flat, (((0,), (0,)), ((), ())), preferred_element_type=jnp.float32
    )
    gain_attn_part = (
        jnp.sum(d_attn_part.astype(jnp.float32) * gathered_attn.astype(jnp.float32), axis=0)
        / gain_attn
    )
    gain_both = gain_reduce(jnp.stack([gain_attn_part, gain_mlp_part]), 3)
    grad_qkv, grad_out_w = grad_reduce([grad_qkv, grad_out_w], 1)
    grad_qkv = grad_qkv.astype(jnp.float32).reshape(model_width, 3, width_local)
    grad_in = grad_in.astype(jnp.float32).reshape(model_width, 2, ff_local)
    grad_out_w = jnp.transpose(grad_out_w.astype(jnp.float32))
    d_norm_attn, gain_both, grad_qkv, grad_out_w, grad_in = lax.optimization_barrier(
        (d_norm_attn, gain_both, grad_qkv, grad_out_w, grad_in)
    )
    d_norm_attn = d_norm_attn.astype(jnp.float32)
    d_rows = d_mid + norm_bwd(d_norm_attn, hat_attn, inv_attn, gain_attn)
    return (
        final_rows[None],
        d_rows[None],
        gain_both[0],
        gain_both[1],
        grad_qkv,
        grad_out_w,
        grad_in,
        grad_down,
    )


def solution(mesh):
    return jax.shard_map(
        shards,
        mesh=mesh,
        in_specs=(
            P("dp", "tensor", None),
            P("dp", None),
            P(),
            P(),
            P(None, None, "tensor"),
            P("tensor", None),
            P(None, None, "tensor"),
            P("tensor", None),
            P("dp", "tensor", None),
        ),
        out_specs=(
            P("dp", "tensor", None),
            P("dp", "tensor", None),
            P("tensor"),
            P("tensor"),
            P(None, None, "tensor"),
            P("tensor", None),
            P(None, None, "tensor"),
            P("tensor", None),
        ),
        check_vma=False,
    )
```

```python
import functools
import math

import jax
import jax.numpy as jnp
from jax import lax
from jax.experimental import pallas as pl
from jax.experimental.pallas import tpu as pltpu
from jax.sharding import PartitionSpec as P

HEAD_DIM = 64


eps_norm = 1e-05
rope_theta = 160000.0
neg_fill = -1e30
sqrt_half = 0.7071067811865476
inv_sqrt_two_pi = 0.3989422804014327


def norm_fwd(rows_f, gain_vec):
    mean_row = jnp.mean(rows_f, axis=-1, keepdims=True)
    centred = rows_f - mean_row
    var_row = jnp.mean(centred * centred, axis=-1, keepdims=True)
    inv_std = lax.rsqrt(var_row + eps_norm)
    hat_rows = centred * inv_std
    return ((hat_rows * gain_vec).astype(jnp.bfloat16), hat_rows, inv_std)


def norm_bwd(grad_norm, hat_rows, inv_std, gain_vec):
    grad_hat = grad_norm * gain_vec
    mean_one = jnp.mean(grad_hat, axis=-1, keepdims=True)
    mean_two = jnp.mean(grad_hat * hat_rows, axis=-1, keepdims=True)
    return inv_std * (grad_hat - mean_one - hat_rows * mean_two)


def half_turn(field_in):
    half_dim = field_in.shape[-1] // 2
    return jnp.concatenate([-field_in[..., half_dim:], field_in[..., :half_dim]], axis=-1)


def positions_of(seg_row):
    before = jnp.sum((seg_row[None, :] < seg_row[:, None]).astype(jnp.int32), axis=1)
    return jnp.arange(seg_row.shape[0], dtype=jnp.int32) - before


def rope_tables(positions, head_dim):
    half_dim = head_dim // 2
    inv_freq = jnp.exp(
        jnp.arange(half_dim, dtype=jnp.float32) * (-2.0 * math.log(rope_theta) / head_dim)
    )
    angles = positions.astype(jnp.float32)[:, None] * inv_freq[None, :]
    cos_tab = jnp.concatenate([jnp.cos(angles), jnp.cos(angles)], axis=-1)
    sin_tab = jnp.concatenate([jnp.sin(angles), jnp.sin(angles)], axis=-1)
    return (cos_tab[None], sin_tab[None])


def rope_apply(field_in, cos_tab, sin_tab):
    return field_in * cos_tab + half_turn(field_in) * sin_tab


def rope_back(grad_in, cos_tab, sin_tab):
    return grad_in * cos_tab - half_turn(grad_in * sin_tab)


def gelu_val(field_in):
    return 0.5 * field_in * (1.0 + lax.erf(field_in * sqrt_half))


def gelu_slope(field_in):
    return (
        0.5 * (1.0 + lax.erf(field_in * sqrt_half))
        + field_in * jnp.exp(-0.5 * field_in * field_in) * inv_sqrt_two_pi
    )


def masked_scores(queries, key_rows, seg_row):
    scale_val = 1.0 / math.sqrt(queries.shape[2])
    scores = jnp.einsum("hqd,hkd->hqk", queries, key_rows, preferred_element_type=jnp.float32)
    same_doc = seg_row[:, None] == seg_row[None, :]
    return jnp.where(same_doc[None], scores * scale_val, neg_fill)


def attend_fwd(queries, key_rows, value_rows, seg_row):
    scores = masked_scores(queries, key_rows, seg_row)
    row_top = jnp.max(scores, axis=-1, keepdims=True)
    exp_vals = jnp.exp(scores - row_top)
    row_total = jnp.sum(exp_vals, axis=-1, keepdims=True)
    prob_bf = (exp_vals / row_total).astype(jnp.bfloat16)
    att_out = jnp.einsum(
        "hqk,hkd->hqd", prob_bf, value_rows, preferred_element_type=jnp.float32
    ).astype(jnp.bfloat16)
    return (att_out, (row_top + jnp.log(row_total))[..., 0])


def attend_bwd(queries, key_rows, value_rows, seg_row, att_out, grad_att, lse_rows):
    scale_val = 1.0 / math.sqrt(queries.shape[2])
    delta_rows = jnp.sum(grad_att.astype(jnp.float32) * att_out.astype(jnp.float32), axis=-1)
    scores = masked_scores(queries, key_rows, seg_row)
    prob_f = jnp.exp(scores - lse_rows[:, :, None])
    grad_prob = jnp.einsum("hqd,hkd->hqk", grad_att, value_rows, preferred_element_type=jnp.float32)
    score_bf = (prob_f * (grad_prob - delta_rows[:, :, None])).astype(jnp.bfloat16)
    prob_bf = prob_f.astype(jnp.bfloat16)
    grad_value = jnp.einsum("hqk,hqd->hkd", prob_bf, grad_att, preferred_element_type=jnp.float32)
    grad_key = (
        jnp.einsum("hqk,hqd->hkd", score_bf, queries, preferred_element_type=jnp.float32) * scale_val
    )
    grad_query = (
        jnp.einsum("hqk,hkd->hqd", score_bf, key_rows, preferred_element_type=jnp.float32) * scale_val
    )
    return (grad_query, grad_key, grad_value)


def heads_first(field_in, head_local):
    return jnp.transpose(field_in.reshape(field_in.shape[0], head_local, HEAD_DIM), (1, 0, 2))


def rows_first(field_in):
    return jnp.transpose(field_in, (1, 0, 2)).reshape(field_in.shape[1], -1)


def bit_orders(n_dp):
    bits = [1 << i for i in range(n_dp.bit_length() - 1)]
    rest = bits[1:]
    turn = len(rest) // 2
    return (bits, bits[:1] + rest[turn:] + rest[:turn])


def grad_reduce_kernel(n_dp, n_arr, *refs):
    orders = bit_orders(n_dp)
    n_stage = len(orders[0])
    x_refs = refs[:n_arr]
    out_refs = refs[n_arr : 2 * n_arr]
    pos = 2 * n_arr
    gath = refs[pos : pos + n_arr]
    pos += n_arr
    recv = [refs[pos + s * n_arr : pos + (s + 1) * n_arr] for s in range(n_stage)]
    pos += n_stage * n_arr
    work = [refs[pos + s * n_arr : pos + (s + 1) * n_arr] for s in range(n_stage - 1)]
    pos += (n_stage - 1) * n_arr
    send_sem, recv_sem = refs[pos], refs[pos + 1]
    me = lax.axis_index("dp")
    mine = lax.axis_index("tensor")

    def bit_of(bit):
        return lax.rem(me // bit, 2)

    def partner_of(bit):
        return me + bit - 2 * bit * bit_of(bit)

    def remote(src, dst, step, half, arr, bit):
        return pltpu.make_async_remote_copy(
            src_ref=src,
            dst_ref=dst,
            send_sem=send_sem.at[step, half, arr],
            recv_sem=recv_sem.at[step, half, arr],
            device_id=(partner_of(bit), mine),
            device_id_type=pl.DeviceIdType.MESH,
        )

    barrier = pltpu.get_barrier_semaphore()
    for bit in orders[0]:
        pl.semaphore_signal(
            barrier, inc=1, device_id=(partner_of(bit), mine), device_id_type=pl.DeviceIdType.MESH
        )
    pl.semaphore_wait(barrier, n_stage)

    offs = [[0], [0]]
    for stage in range(n_stage):
        size = n_dp >> (stage + 1)
        copies = []
        for half in range(2):
            bit = orders[half][stage]
            offs[half].append(offs[half][-1] + bit_of(bit) * size)
            for arr in range(n_arr):
                src = x_refs[arr] if stage == 0 else work[stage - 1][arr]
                away = (1 - bit_of(bit)) * size
                copies.append(
                    remote(
                        src.at[half, pl.ds(away, size)],
                        recv[stage][arr].at[half],
                        stage,
                        half,
                        arr,
                        bit,
                    )
                )
                copies[-1].start()
        for half in range(2):
            kept = bit_of(orders[half][stage]) * size
            for arr in range(n_arr):
                copies[half * n_arr + arr].wait_recv()
                src = x_refs[arr] if stage == 0 else work[stage - 1][arr]
                last = stage == n_stage - 1
                base = offs[half][-1] if last else 0
                dst = gath[arr] if last else work[stage][arr]

                def add_one(i, carry, src=src, dst=dst, kept=kept, base=base, half=half, arr=arr):
                    total = src[half, kept + i].astype(jnp.float32) + recv[stage][arr][
                        half, i
                    ].astype(jnp.float32)
                    dst[half, base + i] = total.astype(jnp.bfloat16)
                    return carry

                lax.fori_loop(0, size, add_one, 0)
        for copy in copies:
            copy.wait_send()
    for stage in reversed(range(n_stage)):
        size = n_dp >> (stage + 1)
        copies = []
        for half in range(2):
            bit = orders[half][stage]
            start = offs[half][stage + 1]
            for arr in range(n_arr):
                part = gath[arr].at[half, pl.ds(start, size)]
                copies.append(remote(part, part, n_stage + stage, half, arr, bit))
                copies[-1].start()
        for copy in copies:
            copy.wait()
    for arr in range(n_arr):
        for half in range(2):

            def move_one(i, carry, arr=arr, half=half):
                out_refs[arr][half, i] = gath[arr][half, i]
                return carry

            lax.fori_loop(0, n_dp, move_one, 0)


def grad_reduce(grads, call_id):
    n_dp = lax.axis_size("dp")
    rows = grads[0].shape[0]
    if n_dp < 4 or n_dp & (n_dp - 1) or rows % (2 * n_dp):
        return [lax.psum(g.astype(jnp.bfloat16), "dp") for g in grads]
    n_arr = len(grads)
    n_stage = n_dp.bit_length() - 1
    part = rows // (2 * n_dp)
    cols = [g.shape[1] for g in grads]
    args = [g.astype(jnp.bfloat16).reshape(2, n_dp, part, c) for g, c in zip(grads, cols)]
    scratch = [pltpu.VMEM((2, n_dp, part, c), jnp.bfloat16) for c in cols]
    for stage in range(n_stage):
        scratch += [pltpu.VMEM((2, n_dp >> (stage + 1), part, c), jnp.bfloat16) for c in cols]
    for stage in range(n_stage - 1):
        scratch += [pltpu.VMEM((2, n_dp >> (stage + 1), part, c), jnp.bfloat16) for c in cols]
    scratch += [pltpu.SemaphoreType.DMA((2 * n_stage, 2, n_arr))] * 2
    moved = 2 * sum(rows * c for c in cols)
    outs = pl.pallas_call(
        functools.partial(grad_reduce_kernel, n_dp, n_arr),
        out_shape=[jax.ShapeDtypeStruct(a.shape, jnp.bfloat16) for a in args],
        in_specs=[pl.BlockSpec(memory_space=pltpu.VMEM)] * n_arr,
        out_specs=[pl.BlockSpec(memory_space=pltpu.VMEM)] * n_arr,
        scratch_shapes=scratch,
        cost_estimate=pl.CostEstimate(flops=0, bytes_accessed=30 * moved, transcendentals=0),
        compiler_params=pltpu.CompilerParams(
            collective_id=call_id, has_side_effects=True, vmem_limit_bytes=40 << 20
        ),
    )(*args)
    return [o.reshape(rows, c) for o, c in zip(outs, cols)]


def gain_reduce_kernel(n_dp, n_tp, x_ref, out_ref, stage_buf, from_tp, from_dp, t_send, t_recv, d_send, d_recv, c_sem):
    me = lax.axis_index("dp")
    mine = lax.axis_index("tensor")
    mesh_type = pl.DeviceIdType.MESH
    barrier = pltpu.get_barrier_semaphore()
    for k in range(1, n_tp):
        pl.semaphore_signal(
            barrier, inc=1, device_id=(me, lax.rem(mine + k, n_tp)), device_id_type=mesh_type
        )
    for k in range(1, n_dp):
        pl.semaphore_signal(
            barrier, inc=1, device_id=(lax.rem(me + k, n_dp), mine), device_id_type=mesh_type
        )
    pl.semaphore_wait(barrier, n_tp + n_dp - 2)
    copies = []
    for k in range(1, n_tp):
        target = lax.rem(mine + k, n_tp)
        copies.append(
            pltpu.make_async_remote_copy(
                src_ref=x_ref.at[target],
                dst_ref=from_tp.at[k],
                send_sem=t_send.at[k],
                recv_sem=t_recv.at[k],
                device_id=(me, target),
                device_id_type=mesh_type,
            )
        )
        copies[-1].start()
    total = x_ref[mine]
    for k in range(1, n_tp):
        copies[k - 1].wait()
        total = total + from_tp[k]
    stage_buf[...] = total
    local = pltpu.make_async_copy(stage_buf, from_dp.at[0], c_sem)
    local.start()
    local.wait()
    copies = []
    for k in range(1, n_dp):
        copies.append(
            pltpu.make_async_remote_copy(
                src_ref=from_dp.at[0],
                dst_ref=from_dp.at[k],
                send_sem=d_send.at[k],
                recv_sem=d_recv.at[k],
                device_id=(lax.rem(me + k, n_dp), mine),
                device_id_type=mesh_type,
            )
        )
        copies[-1].start()
    for k in range(1, n_dp):
        copies[k - 1].wait()
        total = total + from_dp[k]
    out_ref[...] = total


def gain_reduce(parts, call_id):
    n_dp = lax.axis_size("dp")
    n_tp = lax.axis_size("tensor")
    wide = parts.shape[1] // n_tp
    arg = jnp.transpose(parts.reshape(2, n_tp, wide), (1, 0, 2))
    return pl.pallas_call(
        functools.partial(gain_reduce_kernel, n_dp, n_tp),
        out_shape=jax.ShapeDtypeStruct((2, wide), jnp.float32),
        in_specs=[pl.BlockSpec(memory_space=pltpu.VMEM)],
        out_specs=pl.BlockSpec(memory_space=pltpu.VMEM),
        scratch_shapes=[
            pltpu.VMEM((2, wide), jnp.float32),
            pltpu.VMEM((n_tp, 2, wide), jnp.float32),
            pltpu.VMEM((n_dp, 2, wide), jnp.float32),
            pltpu.SemaphoreType.DMA((n_tp,)),
            pltpu.SemaphoreType.DMA((n_tp,)),
            pltpu.SemaphoreType.DMA((n_dp,)),
            pltpu.SemaphoreType.DMA((n_dp,)),
            pltpu.SemaphoreType.DMA,
        ],
        cost_estimate=pl.CostEstimate(flops=0, bytes_accessed=20 << 20, transcendentals=0),
        compiler_params=pltpu.CompilerParams(collective_id=call_id, has_side_effects=True),
    )(arg)


def shards(hidden_in, segment_ids, gain_attn, gain_mlp, w_qkv, w_out, w_in, w_down, out_grad):
    n_parts = lax.axis_size("tensor")
    shard_rows = hidden_in.shape[1]
    total_rows = shard_rows * n_parts
    model_width = hidden_in.shape[2]
    width_local = w_qkv.shape[2]
    head_local = width_local // HEAD_DIM
    ff_local = w_in.shape[2]
    my_index = lax.axis_index("tensor")
    seg_row = segment_ids[0]
    positions = positions_of(seg_row)
    cos_tab, sin_tab = rope_tables(positions, HEAD_DIM)
    my_seg = lax.dynamic_slice_in_dim(seg_row, my_index * shard_rows, shard_rows, 0)
    valid_rows = (my_seg < total_rows).astype(jnp.float32)
    rows_f = hidden_in[0].astype(jnp.float32)
    normed_attn, hat_attn, inv_attn = norm_fwd(rows_f, gain_attn)
    normed_attn, out_grad = lax.optimization_barrier((normed_attn, out_grad))
    gathered_attn = lax.all_gather(normed_attn, "tensor", axis=0, tiled=True)
    grad_top = out_grad[0].astype(jnp.float32) * valid_rows[:, None]
    grad_all = lax.all_gather(grad_top.astype(jnp.bfloat16), "tensor", axis=0, tiled=True)
    projected = jnp.dot(
        gathered_attn,
        w_qkv.reshape(model_width, 3 * width_local),
        preferred_element_type=jnp.float32,
    )
    query_f, key_f, value_f = (
        heads_first(projected[:, i * width_local : (i + 1) * width_local], head_local)
        for i in range(3)
    )
    queries = rope_apply(query_f, cos_tab, sin_tab).astype(jnp.bfloat16)
    key_rows = rope_apply(key_f, cos_tab, sin_tab).astype(jnp.bfloat16)
    value_rows = value_f.astype(jnp.bfloat16)
    att_out, lse_rows = attend_fwd(queries, key_rows, value_rows, seg_row)
    att_flat = rows_first(att_out)
    att_part = jnp.dot(att_flat, w_out, preferred_element_type=jnp.float32).astype(jnp.bfloat16)
    att_part, grad_all = lax.optimization_barrier((att_part, grad_all))
    att_sum = lax.psum_scatter(
        att_part,
        "tensor",
        scatter_dimension=0,
        tiled=True,
    ).astype(jnp.float32)
    mid_rows = rows_f + att_sum
    normed_mlp, hat_mlp, inv_mlp = norm_fwd(mid_rows, gain_mlp)
    gathered_mlp = lax.all_gather(normed_mlp, "tensor", axis=0, tiled=True)
    pre_act = jnp.dot(
        gathered_mlp, w_in.reshape(model_width, 2 * ff_local), preferred_element_type=jnp.float32
    )
    pre_act = pre_act.reshape(total_rows, 2, ff_local)
    up_part = pre_act[:, 0]
    gate_part = pre_act[:, 1]
    act_up = gelu_val(up_part)
    mixed_act = (act_up * gate_part).astype(jnp.bfloat16)
    mlp_part = jnp.dot(mixed_act, w_down, preferred_element_type=jnp.float32).astype(jnp.bfloat16)
    d_mixed = lax.dot_general(
        grad_all, w_down, (((1,), (1,)), ((), ())), preferred_element_type=jnp.float32
    )
    d_up = d_mixed * gate_part * gelu_slope(up_part)
    d_gate = d_mixed * act_up
    d_pre = jnp.stack([d_up, d_gate], axis=1).astype(jnp.bfloat16)
    d_norm_part = lax.dot_general(
        d_pre, w_in, (((1, 2), (1, 2)), ((), ())), preferred_element_type=jnp.float32
    ).astype(jnp.bfloat16)
    d_norm_part, d_pre = lax.optimization_barrier((d_norm_part, d_pre))
    d_norm_mlp = lax.psum_scatter(d_norm_part, "tensor", scatter_dimension=0, tiled=True)
    grad_down = lax.dot_general(
        grad_all, mixed_act, (((0,), (0,)), ((), ())), preferred_element_type=jnp.float32
    ).astype(jnp.bfloat16)
    (grad_down,) = grad_reduce([grad_down], 2)
    grad_in = lax.dot_general(
        gathered_mlp,
        d_pre.reshape(total_rows, 2 * ff_local),
        (((0,), (0,)), ((), ())),
        preferred_element_type=jnp.float32,
    ).astype(jnp.bfloat16)
    d_norm_mlp, grad_in, grad_down, mlp_part = lax.optimization_barrier(
        (d_norm_mlp, grad_in, grad_down, mlp_part)
    )
    d_norm_mlp = d_norm_mlp.astype(jnp.float32)
    gain_mlp_part = jnp.sum(d_norm_mlp * hat_mlp, axis=0)
    d_mid = grad_top + norm_bwd(d_norm_mlp, hat_mlp, inv_mlp, gain_mlp)
    d_mid_bf, grad_in, mlp_part = lax.optimization_barrier(
        (d_mid.astype(jnp.bfloat16), grad_in, mlp_part)
    )
    d_mid_all = lax.all_gather(d_mid_bf, "tensor", axis=0, tiled=True)
    mlp_sum = lax.psum_scatter(mlp_part, "tensor", scatter_dimension=0, tiled=True)
    (grad_in,) = grad_reduce([grad_in], 0)
    grad_down = jnp.transpose(grad_down.astype(jnp.float32))
    d_mid_all, grad_in, grad_down = lax.optimization_barrier((d_mid_all, grad_in, grad_down))
    d_att = lax.dot_general(
        d_mid_all, w_out, (((1,), (1,)), ((), ())), preferred_element_type=jnp.float32
    )
    d_att = heads_first(d_att.astype(jnp.bfloat16), head_local)
    grad_query, grad_key, grad_value = attend_bwd(
        queries, key_rows, value_rows, seg_row, att_out, d_att, lse_rows
    )
    grad_query = rope_back(grad_query, cos_tab, sin_tab)
    grad_key = rope_back(grad_key, cos_tab, sin_tab)
    d_proj = jnp.concatenate(
        [rows_first(g.astype(jnp.bfloat16)) for g in (grad_query, grad_key, grad_value)], axis=1
    )
    d_attn_part = lax.dot_general(
        d_proj,
        w_qkv.reshape(model_width, 3 * width_local),
        (((1,), (1,)), ((), ())),
        preferred_element_type=jnp.float32,
    ).astype(jnp.bfloat16)
    grad_out_w = lax.dot_general(
        d_mid_all, att_flat, (((0,), (0,)), ((), ())), preferred_element_type=jnp.float32
    )
    (grad_out_w,) = grad_reduce([grad_out_w], 4)
    grad_out_w = jnp.transpose(grad_out_w.astype(jnp.float32))
    grad_in = grad_in.astype(jnp.float32).reshape(model_width, 2, ff_local)
    d_attn_part, mlp_sum, d_proj, grad_out_w, grad_in = lax.optimization_barrier(
        (d_attn_part, mlp_sum, d_proj, grad_out_w, grad_in)
    )
    final_rows = (mid_rows + mlp_sum.astype(jnp.float32)).astype(jnp.bfloat16)
    d_norm_attn = lax.psum_scatter(d_attn_part, "tensor", scatter_dimension=0, tiled=True)
    grad_qkv = lax.dot_general(
        gathered_attn,
        d_proj,
        (((0,), (0,)), ((), ())),
        preferred_element_type=jnp.float32,
    )
    gain_attn_part = (
        jnp.sum(d_attn_part.astype(jnp.float32) * gathered_attn.astype(jnp.float32), axis=0)
        / gain_attn
    )
    gain_both = gain_reduce(jnp.stack([gain_attn_part, gain_mlp_part]), 3)
    (grad_qkv,) = grad_reduce([grad_qkv], 1)
    grad_qkv = grad_qkv.astype(jnp.float32).reshape(model_width, 3, width_local)
    d_norm_attn, gain_both, grad_qkv = lax.optimization_barrier((d_norm_attn, gain_both, grad_qkv))
    d_norm_attn = d_norm_attn.astype(jnp.float32)
    d_rows = d_mid + norm_bwd(d_norm_attn, hat_attn, inv_attn, gain_attn)
    return (
        final_rows[None],
        d_rows[None],
        gain_both[0],
        gain_both[1],
        grad_qkv,
        grad_out_w,
        grad_in,
        grad_down,
    )


def solution(mesh):
    return jax.shard_map(
        shards,
        mesh=mesh,
        in_specs=(
            P("dp", "tensor", None),
            P("dp", None),
            P(),
            P(),
            P(None, None, "tensor"),
            P("tensor", None),
            P(None, None, "tensor"),
            P("tensor", None),
            P("dp", "tensor", None),
        ),
        out_specs=(
            P("dp", "tensor", None),
            P("dp", "tensor", None),
            P("tensor"),
            P("tensor"),
            P(None, None, "tensor"),
            P("tensor", None),
            P(None, None, "tensor"),
            P("tensor", None),
        ),
        check_vma=False,
    )
```
